32 devices in a mesh: ctx: 4 (over z), head: 8 (over y, x, core).
Axes of the slice: x: 2, y: 2, z: 4, core: 2. Of those that a mesh axis runs over, the one named last changes fastest.
Arguments:
- layer_input: bfloat16 [1024, 4096], P(('ctx', 'head')), may hold values from -6 to 6
- w_query: bfloat16 [4096, 4096], P('ctx', 'head'), may hold values from -0.09375 to 0.09375
- w_key: bfloat16 [4096, 4096], P('ctx', 'head'), may hold values from -0.09375 to 0.09375
- w_value: bfloat16 [4096, 4096], P('ctx', 'head'), may hold values from -0.09375 to 0.09375
- w_out: bfloat16 [4096, 4096], P('head'), may hold values from -0.09375 to 0.09375
- log_decay: float32 [32, 1024], P('head', 'ctx'), may hold values from -2 to 0
- level_gain: float32 [32, 10], P('head'), may hold values from 0.5 to 2
- level_mask: int32 [8, 10], P('ctx'), may hold values 0 or 1
Outputs:
- layer_out: bfloat16 [1024, 4096], P(('ctx', 'head'))
The draws below stay inside these ranges and needn't reach their ends.
All inputs are finite; a program needn't handle non-finite values. No bound on the sum of `level_mask` on one device may be relied on, other than what follows from the above.
Results may differ from the reference program's by a relative error of at most 0.023.
Values may be sent and summed in bfloat16 or wider, within the bound.
A program may use at most 64 MiB of HBM per device.

```python
import math
import jax
import jax.numpy as jnp
from jax import lax

D = 4096
HEAD_COUNT = 32
HEAD_DIM = 128
TOK_DEV = 256
BLOCK = 128
LEVELS = 10
TOKEN_COUNT = 1024
BLOCKS = 8
N_CTX = 4
N_HEAD = 8


def draw_log_decay(key, part):
    random_subkeys = jax.random.split(key, 7)
    fast_share = 0.5
    fast_head = jax.random.uniform(random_subkeys[0], (HEAD_COUNT,)) < fast_share
    fast_rate = jnp.exp(jax.random.uniform(random_subkeys[1], (HEAD_COUNT,), minval=math.log(1.0 / 50.0), maxval=math.log(1.0 / 30.0)))
    slow_rate = 0.5 / TOKEN_COUNT * jnp.exp(jax.random.uniform(random_subkeys[2], (HEAD_COUNT,), minval=-0.7, maxval=0.7))
    decay_rate = jnp.where(fast_head, fast_rate, slow_rate)
    span_count = TOKEN_COUNT // TOK_DEV
    span_factor = jnp.exp(jax.random.uniform(random_subkeys[3], (HEAD_COUNT, span_count), minval=-0.7, maxval=0.7))
    roughness = jnp.exp(jax.random.uniform(random_subkeys[4], (HEAD_COUNT, TOKEN_COUNT), minval=-0.7, maxval=0.7))
    decay_factor = -decay_rate[:, None] * jnp.repeat(span_factor, TOK_DEV, axis=1) * roughness
    spike_position = jax.random.randint(random_subkeys[5], (HEAD_COUNT, 3), 0, TOKEN_COUNT)
    spike_falloff = jnp.log(jax.random.uniform(random_subkeys[6], (HEAD_COUNT, 3), minval=0.5, maxval=0.8))
    spike_events = jnp.arange(TOKEN_COUNT, dtype=jnp.int32)[None, None, :] == spike_position[:, :, None]
    decay_factor = decay_factor + jnp.sum(jnp.where(spike_events, spike_falloff[:, :, None], 0.0), axis=1)
    return decay_factor.astype(jnp.float32)


def plant(values, rng, low, largest):
    index_at = [jax.random.randint(jax.random.fold_in(rng, axis), (), 0, length) for axis, length in enumerate(values.shape)]
    longest = values.shape.index(max(values.shape))
    next_to = index_at[:longest] + [(index_at[longest] + 1) % values.shape[longest]] + index_at[longest + 1:]
    return values.at[tuple(index_at)].set(low).at[tuple(next_to)].set(largest)


def steps_of(rng, dims, cuts, least, largest):
    loudness, own = 1.0, jax.random.fold_in(rng, 6)
    for axis_at, parts in cuts:
        heights = jnp.exp(jax.random.uniform(jax.random.fold_in(own, axis_at), (parts,), jnp.float32, least / len(cuts), largest / len(cuts)))
        loudness = loudness * jnp.repeat(heights, dims[axis_at] // parts).reshape([-1 if axis == axis_at else 1 for axis in range(len(dims))])
    return loudness


def centred(stream_key, extent, deviation, reach, pieces=(), held_as=jnp.bfloat16):
    level = steps_of(stream_key, extent, pieces, -0.22, 0.18) if pieces else 1.0
    values = jax.random.normal(stream_key, extent, jnp.float32) * deviation * level
    return jnp.minimum(jnp.maximum(values, -reach), reach).astype(held_as)


def setup_inputs(seed: int = 0) -> dict:
    arg_keys = jax.random.split(jax.random.key(seed), 9)
    layer_input = centred(arg_keys[0], (TOKEN_COUNT, D), 1.0, 6.0, ((0, 32),))
    w_query = centred(arg_keys[1], (D, D), D ** -0.5, 0.09375, ((0, 4), (1, 8)))
    w_key = centred(arg_keys[2], (D, D), D ** -0.5, 0.09375, ((0, 4), (1, 8)))
    w_value = centred(arg_keys[3], (D, D), D ** -0.5, 0.09375, ((0, 4), (1, 8)))
    w_out = centred(arg_keys[4], (D, D), D ** -0.5, 0.09375, ((0, 8),))
    log_decay = draw_log_decay(jax.random.fold_in(arg_keys[8], 71), 0)
    level_gain = jnp.clip(jnp.exp(math.log(2.0) - 1.3862944 * jax.random.uniform(arg_keys[6], (HEAD_COUNT, LEVELS), jnp.float32) ** steps_of(arg_keys[6], (HEAD_COUNT, LEVELS), ((0, 8),), -0.2, 0.2)), 0.5, 2.0)
    level_mask = plant((jax.random.randint(arg_keys[7], (BLOCKS, LEVELS), 0, 4) < 3).astype(jnp.int32), jax.random.fold_in(arg_keys[7], 1), 0, 1)
    return {"layer_input": layer_input, "w_query": w_query, "w_key": w_key, "w_value": w_value, "w_out": w_out, "log_decay": log_decay, "level_gain": level_gain, "level_mask": level_mask}


def levels_of(first, second, count):
    mixed = jnp.bitwise_xor(first, second)
    result = jnp.zeros(mixed.shape, jnp.int32)
    for level_bit in range(count):
        result = result + (mixed >= 2 ** level_bit).astype(jnp.int32)
    return result

def unit_rows(block):
    floated = block.astype(jnp.float32)
    return (floated / jnp.sqrt(lax.optimization_barrier(jnp.sum(floated * floated, axis=-1, keepdims=True)) + 1e-06)).astype(jnp.bfloat16)

def reference(layer_input, w_query, w_key, w_value, w_out, log_decay, level_gain, level_mask):
    float_input = layer_input.astype(jnp.float32)

    def project(weight):
        return jnp.dot(float_input, weight.astype(jnp.float32)).astype(jnp.bfloat16)

    def heads_first(array):
        return jnp.transpose(array.reshape(TOKEN_COUNT, HEAD_COUNT, HEAD_DIM), (1, 0, 2))
    query = heads_first(project(w_query))
    keys = heads_first(project(w_key))
    values = heads_first(project(w_value))
    per_span = TOK_DEV // BLOCK
    bit_count = N_CTX.bit_length() - 1
    span_index = jnp.arange(N_CTX, dtype=jnp.int32)
    blocks = span_index[:, None] * per_span + jnp.arange(per_span, dtype=jnp.int32)[None, :]
    level_range = jnp.arange(LEVELS, dtype=jnp.int32)
    near_levels = levels_of(blocks[:, :, None], blocks[:, None, :], LEVELS)
    near_onehot = (near_levels[..., None] == level_range).astype(jnp.float32)
    bit_range = jnp.arange(bit_count, dtype=jnp.int32)
    powers = jnp.left_shift(jnp.ones_like(bit_range), bit_range)
    partner = jnp.bitwise_xor(span_index[:, None], powers[None, :])
    far_levels = levels_of(blocks[:, :, None], (partner * per_span)[:, None, :], LEVELS)
    far_onehot = (far_levels[..., None] == level_range).astype(jnp.float32)
    mask_blocks = level_mask.reshape(N_CTX, per_span, LEVELS).astype(jnp.float32)
    mixed_spans = jnp.bitwise_xor(span_index[:, None], span_index[None, :])
    member = (mixed_spans[..., None] >= powers) & (mixed_spans[..., None] < 2 * powers)
    member = member & (span_index[None, :] < span_index[:, None])[..., None]
    position = jnp.arange(TOK_DEV, dtype=jnp.int32)
    causal = position[:, None] >= position[None, :]

    def one_head(inputs):
        query_head, key_head, value_head, decay_head, gain_head = inputs
        query_unit = unit_rows(query_head.reshape(N_CTX, TOK_DEV, HEAD_DIM))
        key_unit = unit_rows(key_head.reshape(N_CTX, TOK_DEV, HEAD_DIM))
        value_span = value_head.reshape(N_CTX, TOK_DEV, HEAD_DIM).astype(jnp.float32)
        cum = jnp.cumsum(decay_head.reshape(N_CTX, TOK_DEV), axis=1)
        span_total = cum[:, -1]
        block_weight = mask_blocks * gain_head[None, None, :]
        near_block = jnp.einsum('cbl,cbel->cbe', block_weight, near_onehot)
        near_tokens = jnp.repeat(jnp.repeat(near_block, BLOCK, axis=1), BLOCK, axis=2)
        scores = jnp.einsum('ctd,csd->cts', query_unit.astype(jnp.float32), key_unit.astype(jnp.float32))
        spread = cum[:, :, None] - cum[:, None, :]
        decay_factor = jnp.where(causal, jnp.exp(jnp.where(causal, spread, 0.0)), 0.0)
        near_weight = (scores * decay_factor * near_tokens).astype(jnp.bfloat16)
        near_out = jnp.einsum('cts,csd->ctd', near_weight.astype(jnp.float32), value_span)
        decayed_key = (key_unit.astype(jnp.float32) * jnp.exp(span_total[:, None] - cum)[:, :, None]).astype(jnp.bfloat16)
        span_state = jnp.einsum('ctd,cte->cde', decayed_key.astype(jnp.float32), value_span)
        inclusive = jnp.cumsum(span_total)
        between = (inclusive - span_total)[:, None] - inclusive[None, :]
        coeff = jnp.where(member, jnp.exp(jnp.where(member, between[..., None], 0.0)), 0.0)
        carried = jnp.einsum('cnm,nde->cmde', coeff, span_state, precision=lax.Precision.HIGHEST)
        far_block = jnp.einsum('cbl,cbml->cbm', block_weight, far_onehot)
        far_tokens = jnp.repeat(far_block, BLOCK, axis=1)
        scaled = query_unit.astype(jnp.float32) * jnp.exp(cum)[:, :, None]
        reached = jnp.einsum('ctd,cmde->ctme', scaled, carried, precision=lax.Precision.HIGHEST)
        far_out = jnp.einsum('ctme,ctm->cte', reached, far_tokens, precision=lax.Precision.HIGHEST)
        return (near_out + far_out).astype(jnp.bfloat16).reshape(TOKEN_COUNT, HEAD_DIM)
    heads = lax.map(one_head, (query, keys, values, log_decay, level_gain))
    heads_out = jnp.transpose(heads, (1, 0, 2)).reshape(TOKEN_COUNT, D)
    group_width = D // N_HEAD
    grouped = jnp.transpose(heads_out.reshape(TOKEN_COUNT, N_HEAD, group_width), (1, 0, 2))
    weight_groups = w_out.reshape(N_HEAD, group_width, D)

    def add_group(total, pair):
        product = jnp.dot(pair[0].astype(jnp.float32), pair[1].astype(jnp.float32))
        rounded = lax.optimization_barrier(product.astype(jnp.bfloat16)).astype(jnp.float32)
        return (total + rounded, None)
    summed, unused = lax.scan(add_group, jnp.zeros((TOKEN_COUNT, D), jnp.float32), (grouped, weight_groups))
    return summed.astype(jnp.bfloat16)
```

```python
import jax
import jax.numpy as jnp
from jax import lax
from jax.sharding import PartitionSpec as P

HEAD_DIM = 128
BLOCK = 128


def swapped(value, axis, stride):
    mask = 2**stride
    pairs = [(source, source ^ mask) for source in range(lax.axis_size(axis))]
    return lax.ppermute(value, axis, pairs)


def levels_of(first, second, count):
    mixed = jnp.bitwise_xor(first, second)
    result = jnp.zeros(mixed.shape, jnp.int32)
    for level_bit in range(count):
        result = result + (mixed >= 2**level_bit).astype(jnp.int32)
    return result


def unit_rows(block):
    floated = block.astype(jnp.float32)
    return (floated / jnp.sqrt(jnp.sum(floated * floated, axis=-1, keepdims=True) + 1e-06)).astype(
        jnp.bfloat16
    )


def on_device(layer_input, w_query, w_key, w_value, w_out, log_decay, level_gain, level_mask):
    n_ctx = lax.axis_size("ctx")
    rows, model = layer_input.shape
    depth = w_query.shape[0]
    slices = layer_input.reshape(rows, n_ctx, depth).transpose(1, 0, 2)
    mine = lax.all_to_all(slices, "ctx", split_axis=0, concat_axis=0)
    piece = lax.all_gather(mine, "head", axis=1, tiled=True)
    tokens = piece.reshape(n_ctx * piece.shape[1], depth)
    outputs = [
        lax.psum_scatter(
            jnp.dot(tokens, weight, preferred_element_type=jnp.float32).astype(jnp.bfloat16),
            "ctx",
            scatter_dimension=0,
            tiled=True,
        )
        for weight in (w_query, w_key, w_value)
    ]
    joined = jnp.concatenate(outputs, axis=1)
    width = w_query.shape[1]
    local_heads = width // HEAD_DIM
    span = joined.shape[0]
    query_unit = unit_rows(joined[:, :width].reshape(span, local_heads, HEAD_DIM))
    key_unit = unit_rows(joined[:, width : 2 * width].reshape(span, local_heads, HEAD_DIM))
    values = joined[:, 2 * width :].reshape(span, local_heads, HEAD_DIM)
    cum = jnp.cumsum(log_decay, axis=1)
    span_total = cum[:, -1]
    level_count = level_gain.shape[1]
    per_span = span // BLOCK
    ctx_index = lax.axis_index("ctx")
    blocks = ctx_index * per_span + jnp.arange(per_span, dtype=jnp.int32)
    level_range = jnp.arange(level_count, dtype=jnp.int32)
    near_levels = levels_of(blocks[:, None], blocks[None, :], level_count)
    near_onehot = (near_levels[..., None] == level_range).astype(jnp.float32)
    block_weight = level_mask.astype(jnp.float32)[:, None, :] * level_gain[None, :, :]
    near_block = jnp.einsum("bhl,bel->hbe", block_weight, near_onehot)
    scores = jnp.einsum("thd,shd->hts", query_unit, key_unit, preferred_element_type=jnp.float32)
    position = jnp.arange(span, dtype=jnp.int32)
    causal = position[:, None] >= position[None, :]
    spread = cum[:, :, None] - cum[:, None, :]
    decay_factor = jnp.where(causal, jnp.exp(jnp.where(causal, spread, 0.0)), 0.0)
    shaped = (scores * decay_factor).reshape(local_heads, per_span, BLOCK, per_span, BLOCK)
    near_weight = (
        (shaped * near_block[:, :, None, :, None])
        .reshape(local_heads, span, span)
        .astype(jnp.bfloat16)
    )
    near_out = jnp.einsum("hts,shd->thd", near_weight, values, preferred_element_type=jnp.float32)
    decayed_key = (
        key_unit.astype(jnp.float32) * jnp.exp(span_total[None, :] - cum.T)[:, :, None]
    ).astype(jnp.bfloat16)
    span_state = jnp.einsum("thd,the->hde", decayed_key, values, preferred_element_type=jnp.float32)
    bit_count = lax.axis_size("ctx").bit_length() - 1
    bit_range = jnp.arange(bit_count, dtype=jnp.int32)
    powers = jnp.left_shift(jnp.ones_like(bit_range), bit_range)
    group_total, group_state = (span_total, span_state)
    before = jnp.zeros_like(span_total)
    collected = []
    for bit_index in range(bit_count):
        other_total, other_state = (
            swapped(group_total.astype(jnp.bfloat16), "ctx", bit_index).astype(group_total.dtype),
            swapped(group_state.astype(jnp.bfloat16), "ctx", bit_index).astype(group_state.dtype),
        )
        upper = jnp.bitwise_and(jnp.right_shift(ctx_index, bit_index), 1) == 1
        collected.append(jnp.where(upper, jnp.exp(before)[:, None, None] * other_state, 0.0))
        lower_total = jnp.where(upper, other_total, group_total)
        higher_total = jnp.where(upper, group_total, other_total)
        lower_state = jnp.where(upper, other_state, group_state)
        higher_state = jnp.where(upper, group_state, other_state)
        group_state = jnp.exp(higher_total)[:, None, None] * lower_state + higher_state
        group_total = lower_total + higher_total
        before = before + jnp.where(upper, other_total, 0.0)
    carried = jnp.stack(collected, axis=0)
    partner = jnp.bitwise_xor(ctx_index, powers)
    far_levels = levels_of(blocks[:, None], (partner * per_span)[None, :], level_count)
    far_onehot = (far_levels[..., None] == level_range).astype(jnp.float32)
    far_block = jnp.einsum("bhl,bml->bhm", block_weight, far_onehot)
    far_tokens = jnp.repeat(far_block, BLOCK, axis=0)
    scaled = query_unit.astype(jnp.float32) * jnp.exp(cum.T)[:, :, None]
    reached = jnp.einsum("thd,mhde->thme", scaled, carried, precision=lax.Precision.HIGHEST)
    far_out = jnp.einsum("thme,thm->the", reached, far_tokens, precision=lax.Precision.HIGHEST)
    heads_out = (near_out + far_out).astype(jnp.bfloat16).reshape(span, width)
    return lax.psum_scatter(
        jnp.dot(heads_out, w_out, preferred_element_type=jnp.float32).astype(jnp.bfloat16),
        "head",
        scatter_dimension=0,
        tiled=True,
    )


def solution(mesh):
    in_specs = (
        P(("ctx", "head"), None),
        P("ctx", "head"),
        P("ctx", "head"),
        P("ctx", "head"),
        P("head", None),
        P("head", "ctx"),
        P("head", None),
        P("ctx", None),
    )
    out_specs = P(("ctx", "head"), None)
    return jax.shard_map(
        on_device, mesh=mesh, in_specs=in_specs, out_specs=out_specs, check_vma=False
    )
```

```python
import functools

import jax
import jax.numpy as jnp
from jax import lax
from jax.experimental import pallas as pl
from jax.experimental.pallas import tpu as pltpu
from jax.sharding import PartitionSpec as P

HEAD_DIM = 128
BLOCK = 128
MESH = pl.DeviceIdType.MESH


def flipped(index, mask):
    bit = 1
    while bit <= mask:
        if mask & bit:
            index = index + bit - 2 * bit * ((index // bit) % 2)
        bit *= 2
    return index


def subsets(bits):
    masks = [0]
    for bit in bits:
        masks = masks + [mask | bit for mask in masks]
    return masks


def bits_of(count):
    return [2**k for k in range(count.bit_length() - 1)]


def visit(step, me, count):
    after, before = count - 1 - me, me
    extra = jnp.abs(after - before)
    more_after = after > before
    turn = step - extra
    half = turn // 2
    from_end = count - 1 - jnp.where(more_after, extra, 0) - half
    from_start = jnp.where(more_after, 0, extra) + half
    even = turn % 2 == 0
    paired = jnp.where(even == more_after, from_start, from_end)
    lone = jnp.where(more_after, count - 1 - step, step)
    return jnp.where(step < extra, lone, paired)


def project_kernel(
    spans, heads, x_ref, wq_ref, wk_ref, wv_ref, out_ref,
    xs, weight, part, inbox, total,
    w_sem, own_sem, z_send, z_recv, g_send, g_recv, p_send, p_recv,
):
    me, lane = lax.axis_index("ctx"), lax.axis_index("head")
    rows = x_ref.shape[0]
    depth, width = weight.shape[1:]
    bits = bits_of(heads)
    order = [visit(step, me, spans) for step in range(spans - 1)]
    sources = (wq_ref, wk_ref, wv_ref)
    loads = [pltpu.make_async_copy(ref, weight.at[k], w_sem.at[k]) for k, ref in enumerate(sources)]

    def columns(span):
        return x_ref.at[:, pl.ds(pl.multiple_of(span * depth, depth), depth)]

    own = pltpu.make_async_copy(columns(me), xs.at[me, lane], own_sem)
    own.start()
    for load in loads:
        load.start()
    barrier = pltpu.get_barrier_semaphore()
    for ahead in range(1, spans):
        pl.semaphore_signal(barrier, inc=1, device_id={"ctx": lax.rem(me + ahead, spans)}, device_id_type=MESH)
    for bit in bits:
        pl.semaphore_signal(barrier, inc=1, device_id={"head": flipped(lane, bit)}, device_id_type=MESH)
    pl.semaphore_wait(barrier, spans - 1 + len(bits))

    def exchange(span, source):
        return pltpu.make_async_remote_copy(
            src_ref=columns(span), dst_ref=xs.at[source, lane],
            send_sem=z_send.at[span], recv_sem=z_recv.at[source],
            device_id={"ctx": span}, device_id_type=MESH,
        )

    for span in order:
        exchange(span, me).start()

    def gather(span, mask, bit):
        block = xs.at[span, flipped(lane, mask)]
        return pltpu.make_async_remote_copy(
            src_ref=block, dst_ref=block,
            send_sem=g_send.at[span, mask | bit], recv_sem=g_recv.at[span, mask | bit],
            device_id={"head": flipped(lane, bit)}, device_id_type=MESH,
        )

    def settled(span, mask):
        block = xs.at[span, flipped(lane, mask)]
        return pltpu.make_async_remote_copy(
            src_ref=block, dst_ref=block,
            send_sem=g_send.at[span, mask], recv_sem=g_recv.at[span, mask],
            device_id={"head": flipped(lane, bits[0])}, device_id_type=MESH,
        )

    def to_right(span, k):
        return pltpu.make_async_remote_copy(
            src_ref=part.at[span, k], dst_ref=inbox.at[span, k],
            send_sem=p_send.at[span, k], recv_sem=p_recv.at[span, k],
            device_id={"ctx": lax.rem(me + 1, spans)}, device_id_type=MESH,
        )

    def to_left(span, k):
        slot = jnp.where(span == me - 1, spans, span)
        return pltpu.make_async_remote_copy(
            src_ref=part.at[span, k], dst_ref=inbox.at[slot, k],
            send_sem=p_send.at[span, k], recv_sem=p_recv.at[slot, k],
            device_id={"ctx": lax.rem(me + spans - 1, spans)}, device_id_type=MESH,
        )

    def landed(slot, k):
        pltpu.make_async_remote_copy(
            src_ref=inbox.at[slot, k], dst_ref=inbox.at[slot, k],
            send_sem=p_send.at[0, k], recv_sem=p_recv.at[slot, k],
            device_id={"ctx": lax.rem(me + 1, spans)}, device_id_type=MESH,
        ).wait_recv()

    def product(span, k):
        block = xs[span]
        if rows % 16:
            block = block.astype(jnp.float32)
        block = block.reshape(heads * rows, depth).astype(jnp.bfloat16)
        return jnp.dot(block, weight[k], preferred_element_type=jnp.float32)

    queue = [me] + order
    orders = [bits[1:] + bits[:1], bits[:0:-1] + bits[:1]]

    def advance(place, phase):
        span, path = queue[place], orders[place % 2]
        if phase == 0:
            if place == 0:
                own.wait()
            else:
                exchange(span, span).wait_recv()
        else:
            for mask in subsets(path[: phase - 1]):
                settled(span, mask | path[phase - 1]).wait_recv()
        if phase < len(bits):
            for mask in subsets(path[:phase]):
                gather(span, mask, path[phase]).start()

    def compute(place):
        span = queue[place]
        for k in range(3):
            if place == 1:
                loads[k].wait()
            part[span, k] = product(span, k).astype(jnp.bfloat16)

            @pl.when((span > me) & (me == 0))
            def _():
                to_right(span, k).start()

            @pl.when((span < me) & (me == spans - 1))
            def _():
                to_left(span, k).start()

    for wave in range(spans + len(bits)):
        for phase in range(len(bits), -1, -1):
            place = wave - phase
            if 0 <= place < spans:
                advance(place, phase)
                if phase == len(bits) and place > 0:
                    compute(place)
    for k in range(3):
        total[k] = product(me, k)
    for span in order:
        for k in range(3):

            @pl.when((span > me) & (me > 0))
            def _():
                landed(span, k)
                part[span, k] = (part[span, k].astype(jnp.float32) + inbox[span, k].astype(jnp.float32)).astype(jnp.bfloat16)
                to_right(span, k).start()

            @pl.when((span < me) & (me < spans - 1))
            def _():
                landed(span, k)
                part[span, k] = (part[span, k].astype(jnp.float32) + inbox[span, k].astype(jnp.float32)).astype(jnp.bfloat16)
                to_left(span, k).start()

    for k in range(3):

        @pl.when(me > 0)
        def _():
            landed(me, k)
            total[k] = total[k] + inbox[me, k].astype(jnp.float32)

        @pl.when(me < spans - 1)
        def _():
            landed(spans, k)
            total[k] = total[k] + inbox[spans, k].astype(jnp.float32)

        out_ref[k] = total[k].astype(jnp.bfloat16)
    for span in order:
        exchange(span, me).wait_send()
        for k in range(3):
            to_right(span, k).wait_send()
    for span in queue:
        for mask in range(1, heads):
            settled(span, mask).wait_send()


def project(x, w_query, w_key, w_value):
    spans, heads = lax.axis_size("ctx"), lax.axis_size("head")
    rows = x.shape[0]
    depth, width = w_query.shape
    tokens = heads * rows
    dma = pltpu.SemaphoreType.DMA
    hbm = pl.BlockSpec(memory_space=pl.ANY)
    return pl.pallas_call(
        functools.partial(project_kernel, spans, heads),
        out_shape=jax.ShapeDtypeStruct((3, tokens, width), jnp.bfloat16),
        in_specs=[hbm] * 4,
        out_specs=pl.BlockSpec(memory_space=pltpu.VMEM),
        scratch_shapes=[
            pltpu.VMEM((spans, heads, rows, depth), jnp.bfloat16),
            pltpu.VMEM((3, depth, width), jnp.bfloat16),
            pltpu.VMEM((spans, 3, tokens, width), jnp.bfloat16),
            pltpu.VMEM((spans + 1, 3, tokens, width), jnp.bfloat16),
            pltpu.VMEM((3, tokens, width), jnp.float32),
            dma((3,)), dma, dma((spans,)), dma((spans,)),
            dma((spans, heads)), dma((spans, heads)),
            dma((spans, 3)), dma((spans + 1, 3)),
        ],
        compiler_params=pltpu.CompilerParams(collective_id=0, has_side_effects=True),
        name="project",
    )(x, w_query, w_key, w_value)


def output_kernel(heads, heads_ref, w_ref, out_ref, weight, part, inbox, w_sem, s_send, s_recv):
    lane = lax.axis_index("head")
    rows = out_ref.shape[0]
    chunks, chunk = part.shape[0], part.shape[-1]
    bits = bits_of(heads)
    loads = [
        pltpu.make_async_copy(w_ref.at[:, pl.ds(j * chunk, chunk)], weight.at[j], w_sem.at[j])
        for j in range(chunks)
    ]
    for load in loads:
        load.start()
    barrier = pltpu.get_barrier_semaphore()
    for bit in bits:
        pl.semaphore_signal(barrier, inc=1, device_id={"head": flipped(lane, bit)}, device_id_type=MESH)
    pl.semaphore_wait(barrier, len(bits))
    orders = [bits[:1] + bits[1:], bits[:1] + bits[:0:-1]]

    def transfer(j, phase, mask):
        bit = orders[j % 2][phase]
        return pltpu.make_async_remote_copy(
            src_ref=part.at[j, flipped(lane, mask | bit)], dst_ref=inbox.at[j, phase, mask],
            send_sem=s_send.at[j, phase, mask], recv_sem=s_recv.at[j, phase, mask],
            device_id={"head": flipped(lane, bit)}, device_id_type=MESH,
        )

    def advance(j, phase):
        path = orders[j % 2]
        if phase == 0:
            loads[j].wait()
            product = jnp.dot(heads_ref[...], weight[j], preferred_element_type=jnp.float32)
            part[j] = product.reshape(heads, rows, chunk).astype(jnp.bfloat16)
        else:
            for mask in subsets(path[phase:]):
                transfer(j, phase - 1, mask).wait_recv()
                place = flipped(lane, mask)
                added = part[j, place].astype(jnp.float32) + inbox[j, phase - 1, mask].astype(jnp.float32)
                if phase < len(bits):
                    part[j, place] = added.astype(jnp.bfloat16)
                else:
                    out_ref[:, pl.ds(j * chunk, chunk)] = added.astype(jnp.bfloat16)
        if phase < len(bits):
            for mask in subsets(path[phase + 1 :]):
                transfer(j, phase, mask).start()

    for wave in range(chunks + len(bits)):
        for phase in range(len(bits), -1, -1):
            if 0 <= wave - phase < chunks:
                advance(wave - phase, phase)
    for j in range(chunks):
        for phase in range(len(bits)):
            for mask in subsets(orders[j % 2][phase + 1 :]):
                transfer(j, phase, mask).wait_send()


def output(heads_out, w_out):
    heads = lax.axis_size("head")
    tokens, width = heads_out.shape
    model = w_out.shape[1]
    rows = tokens // heads
    chunks = 4
    chunk = model // chunks
    phases = heads.bit_length() - 1
    dma = pltpu.SemaphoreType.DMA
    return pl.pallas_call(
        functools.partial(output_kernel, heads),
        out_shape=jax.ShapeDtypeStruct((rows, model), jnp.bfloat16),
        in_specs=[pl.BlockSpec(memory_space=pltpu.VMEM), pl.BlockSpec(memory_space=pl.ANY)],
        out_specs=pl.BlockSpec(memory_space=pltpu.VMEM),
        scratch_shapes=[
            pltpu.VMEM((chunks, width, chunk), jnp.bfloat16),
            pltpu.VMEM((chunks, heads, rows, chunk), jnp.bfloat16),
            pltpu.VMEM((chunks, phases, heads, rows, chunk), jnp.bfloat16),
            dma((chunks,)), dma((chunks, phases, heads)), dma((chunks, phases, heads)),
        ],
        compiler_params=pltpu.CompilerParams(collective_id=1, has_side_effects=True),
        name="output",
    )(heads_out, w_out)


def swapped(value, axis, stride):
    mask = 2**stride
    pairs = [(source, source ^ mask) for source in range(lax.axis_size(axis))]
    return lax.ppermute(value, axis, pairs)


def levels_of(first, second, count):
    mixed = jnp.bitwise_xor(first, second)
    result = jnp.zeros(mixed.shape, jnp.int32)
    for level_bit in range(count):
        result = result + (mixed >= 2**level_bit).astype(jnp.int32)
    return result


def unit_rows(block):
    floated = block.astype(jnp.float32)
    return (floated / jnp.sqrt(jnp.sum(floated * floated, axis=-1, keepdims=True) + 1e-06)).astype(
        jnp.bfloat16
    )


def on_device(layer_input, w_query, w_key, w_value, w_out, log_decay, level_gain, level_mask):
    joined = project(layer_input, w_query, w_key, w_value)
    width = w_query.shape[1]
    local_heads = width // HEAD_DIM
    span = joined.shape[1]
    query_unit = unit_rows(joined[0].reshape(span, local_heads, HEAD_DIM))
    key_unit = unit_rows(joined[1].reshape(span, local_heads, HEAD_DIM))
    values = joined[2].reshape(span, local_heads, HEAD_DIM)
    cum = jnp.cumsum(log_decay, axis=1)
    span_total = cum[:, -1]
    level_count = level_gain.shape[1]
    per_span = span // BLOCK
    ctx_index = lax.axis_index("ctx")
    blocks = ctx_index * per_span + jnp.arange(per_span, dtype=jnp.int32)
    level_range = jnp.arange(level_count, dtype=jnp.int32)
    near_levels = levels_of(blocks[:, None], blocks[None, :], level_count)
    near_onehot = (near_levels[..., None] == level_range).astype(jnp.float32)
    block_weight = level_mask.astype(jnp.float32)[:, None, :] * level_gain[None, :, :]
    near_block = jnp.einsum("bhl,bel->hbe", block_weight, near_onehot)
    scores = jnp.einsum("thd,shd->hts", query_unit, key_unit, preferred_element_type=jnp.float32)
    position = jnp.arange(span, dtype=jnp.int32)
    causal = position[:, None] >= position[None, :]
    spread = cum[:, :, None] - cum[:, None, :]
    decay_factor = jnp.where(causal, jnp.exp(jnp.where(causal, spread, 0.0)), 0.0)
    shaped = (scores * decay_factor).reshape(local_heads, per_span, BLOCK, per_span, BLOCK)
    near_weight = (
        (shaped * near_block[:, :, None, :, None])
        .reshape(local_heads, span, span)
        .astype(jnp.bfloat16)
    )
    near_out = jnp.einsum("hts,shd->thd", near_weight, values, preferred_element_type=jnp.float32)
    decayed_key = (
        key_unit.astype(jnp.float32) * jnp.exp(span_total[None, :] - cum.T)[:, :, None]
    ).astype(jnp.bfloat16)
    span_state = jnp.einsum("thd,the->hde", decayed_key, values, preferred_element_type=jnp.float32)
    bit_count = lax.axis_size("ctx").bit_length() - 1
    bit_range = jnp.arange(bit_count, dtype=jnp.int32)
    powers = jnp.left_shift(jnp.ones_like(bit_range), bit_range)
    group_total, group_state = (span_total, span_state)
    before = jnp.zeros_like(span_total)
    collected = []
    for bit_index in range(bit_count):
        other_total, other_state = (
            swapped(group_total.astype(jnp.bfloat16), "ctx", bit_index).astype(group_total.dtype),
            swapped(group_state.astype(jnp.bfloat16), "ctx", bit_index).astype(group_state.dtype),
        )
        upper = jnp.bitwise_and(jnp.right_shift(ctx_index, bit_index), 1) == 1
        collected.append(jnp.where(upper, jnp.exp(before)[:, None, None] * other_state, 0.0))
        lower_total = jnp.where(upper, other_total, group_total)
        higher_total = jnp.where(upper, group_total, other_total)
        lower_state = jnp.where(upper, other_state, group_state)
        higher_state = jnp.where(upper, group_state, other_state)
        group_state = jnp.exp(higher_total)[:, None, None] * lower_state + higher_state
        group_total = lower_total + higher_total
        before = before + jnp.where(upper, other_total, 0.0)
    carried = jnp.stack(collected, axis=0)
    partner = jnp.bitwise_xor(ctx_index, powers)
    far_levels = levels_of(blocks[:, None], (partner * per_span)[None, :], level_count)
    far_onehot = (far_levels[..., None] == level_range).astype(jnp.float32)
    far_block = jnp.einsum("bhl,bml->bhm", block_weight, far_onehot)
    far_tokens = jnp.repeat(far_block, BLOCK, axis=0)
    scaled = query_unit.astype(jnp.float32) * jnp.exp(cum.T)[:, :, None]
    reached = jnp.einsum("thd,mhde->thme", scaled, carried, precision=lax.Precision.HIGHEST)
    far_out = jnp.einsum("thme,thm->the", reached, far_tokens, precision=lax.Precision.HIGHEST)
    heads_out = (near_out + far_out).astype(jnp.bfloat16).reshape(span, width)
    return output(heads_out, w_out)


def solution(mesh):
    in_specs = (
        P(("ctx", "head"), None),
        P("ctx", "head"),
        P("ctx", "head"),
        P("ctx", "head"),
        P("head", None),
        P("head", "ctx"),
        P("head", None),
        P("ctx", None),
    )
    out_specs = P(("ctx", "head"), None)
    return jax.shard_map(
        on_device, mesh=mesh, in_specs=in_specs, out_specs=out_specs, check_vma=False
    )
```

```python
import functools

import jax
import jax.numpy as jnp
from jax import lax
from jax.experimental import pallas as pl
from jax.experimental.pallas import tpu as pltpu
from jax.sharding import PartitionSpec as P

HEAD_DIM = 128
BLOCK = 128
MESH = pl.DeviceIdType.MESH


def flipped(index, mask):
    bit = 1
    while bit <= mask:
        if mask & bit:
            index = index + bit - 2 * bit * ((index // bit) % 2)
        bit *= 2
    return index


def subsets(bits):
    masks = [0]
    for bit in bits:
        masks = masks + [mask | bit for mask in masks]
    return masks


def bits_of(count):
    return [2**k for k in range(count.bit_length() - 1)]


def visit(step, me, count):
    after, before = count - 1 - me, me
    extra = jnp.abs(after - before)
    more_after = after > before
    turn = step - extra
    half = turn // 2
    from_end = count - 1 - jnp.where(more_after, extra, 0) - half
    from_start = jnp.where(more_after, 0, extra) + half
    even = turn % 2 == 0
    paired = jnp.where(even == more_after, from_start, from_end)
    lone = jnp.where(more_after, count - 1 - step, step)
    return jnp.where(step < extra, lone, paired)


def project_kernel(
    spans, heads, x_ref, wq_ref, wk_ref, wv_ref, out_ref,
    xs, weight, part, inbox, total,
    w_sem, own_sem, z_send, z_recv, g_send, g_recv, p_send, p_recv,
):
    me, lane = lax.axis_index("ctx"), lax.axis_index("head")
    rows = x_ref.shape[0]
    depth, width = weight.shape[1:]
    bits = bits_of(heads)
    order = [visit(step, me, spans) for step in range(spans - 1)]
    sources = (wq_ref, wk_ref, wv_ref)
    loads = [pltpu.make_async_copy(ref, weight.at[k], w_sem.at[k]) for k, ref in enumerate(sources)]

    def columns(span):
        return x_ref.at[:, pl.ds(pl.multiple_of(span * depth, depth), depth)]

    own = pltpu.make_async_copy(columns(me), xs.at[me, lane], own_sem)
    own.start()
    for load in loads:
        load.start()
    barrier = pltpu.get_barrier_semaphore()
    for ahead in range(1, spans):
        pl.semaphore_signal(barrier, inc=1, device_id={"ctx": lax.rem(me + ahead, spans)}, device_id_type=MESH)
    for bit in bits:
        pl.semaphore_signal(barrier, inc=1, device_id={"head": flipped(lane, bit)}, device_id_type=MESH)
    pl.semaphore_wait(barrier, spans - 1 + len(bits))

    def exchange(span, source):
        return pltpu.make_async_remote_copy(
            src_ref=columns(span), dst_ref=xs.at[source, lane],
            send_sem=z_send.at[span], recv_sem=z_recv.at[source],
            device_id={"ctx": span}, device_id_type=MESH,
        )

    for span in order:
        exchange(span, me).start()

    def gather(span, mask, bit):
        block = xs.at[span, flipped(lane, mask)]
        return pltpu.make_async_remote_copy(
            src_ref=block, dst_ref=block,
            send_sem=g_send.at[span, mask | bit], recv_sem=g_recv.at[span, mask | bit],
            device_id={"head": flipped(lane, bit)}, device_id_type=MESH,
        )

    def settled(span, mask):
        block = xs.at[span, flipped(lane, mask)]
        return pltpu.make_async_remote_copy(
            src_ref=block, dst_ref=block,
            send_sem=g_send.at[span, mask], recv_sem=g_recv.at[span, mask],
            device_id={"head": flipped(lane, bits[0])}, device_id_type=MESH,
        )

    def to_right(span, k):
        return pltpu.make_async_remote_copy(
            src_ref=part.at[span, k], dst_ref=inbox.at[span, k],
            send_sem=p_send.at[span, k], recv_sem=p_recv.at[span, k],
            device_id={"ctx": lax.rem(me + 1, spans)}, device_id_type=MESH,
        )

    def to_left(span, k):
        slot = jnp.where(span == me - 1, spans, span)
        return pltpu.make_async_remote_copy(
            src_ref=part.at[span, k], dst_ref=inbox.at[slot, k],
            send_sem=p_send.at[span, k], recv_sem=p_recv.at[slot, k],
            device_id={"ctx": lax.rem(me + spans - 1, spans)}, device_id_type=MESH,
        )

    def landed(slot, k):
        pltpu.make_async_remote_copy(
            src_ref=inbox.at[slot, k], dst_ref=inbox.at[slot, k],
            send_sem=p_send.at[0, k], recv_sem=p_recv.at[slot, k],
            device_id={"ctx": lax.rem(me + 1, spans)}, device_id_type=MESH,
        ).wait_recv()

    def product(span, k):
        block = xs[span]
        if rows % 16:
            block = block.astype(jnp.float32)
        block = block.reshape(heads * rows, depth).astype(jnp.bfloat16)
        return jnp.dot(block, weight[k], preferred_element_type=jnp.float32)

    queue = [me] + order
    orders = [bits[1:] + bits[:1], bits[:0:-1] + bits[:1]]

    def advance(place, phase):
        span, path = queue[place], orders[place % 2]
        if phase == 0:
            if place == 0:
                own.wait()
            else:
                exchange(span, span).wait_recv()
        else:
            for mask in subsets(path[: phase - 1]):
                settled(span, mask | path[phase - 1]).wait_recv()
        if phase < len(bits):
            for mask in subsets(path[:phase]):
                gather(span, mask, path[phase]).start()

    def compute(place):
        span = queue[place]
        for k in range(3):
            if place == 1:
                loads[k].wait()
            part[span, k] = product(span, k).astype(jnp.bfloat16)

            @pl.when((span > me) & (me == 0))
            def _():
                to_right(span, k).start()

            @pl.when((span < me) & (me == spans - 1))
            def _():
                to_left(span, k).start()

    for wave in range(spans + len(bits)):
        for phase in range(len(bits), -1, -1):
            place = wave - phase
            if 0 <= place < spans:
                advance(place, phase)
                if phase == len(bits) and place > 0:
                    compute(place)
    for k in range(3):
        total[k] = product(me, k)
    for span in order:
        for k in range(3):

            @pl.when((span > me) & (me > 0))
            def _():
                landed(span, k)
                part[span, k] = (part[span, k].astype(jnp.float32) + inbox[span, k].astype(jnp.float32)).astype(jnp.bfloat16)
                to_right(span, k).start()

            @pl.when((span < me) & (me < spans - 1))
            def _():
                landed(span, k)
                part[span, k] = (part[span, k].astype(jnp.float32) + inbox[span, k].astype(jnp.float32)).astype(jnp.bfloat16)
                to_left(span, k).start()

    for k in range(3):

        @pl.when(me > 0)
        def _():
            landed(me, k)
            total[k] = total[k] + inbox[me, k].astype(jnp.float32)

        @pl.when(me < spans - 1)
        def _():
            landed(spans, k)
            total[k] = total[k] + inbox[spans, k].astype(jnp.float32)

        out_ref[k] = total[k].astype(jnp.bfloat16)
    for span in order:
        exchange(span, me).wait_send()
        for k in range(3):
            to_right(span, k).wait_send()
    for span in queue:
        for mask in range(1, heads):
            settled(span, mask).wait_send()


def project(x, w_query, w_key, w_value):
    spans, heads = lax.axis_size("ctx"), lax.axis_size("head")
    rows = x.shape[0]
    depth, width = w_query.shape
    tokens = heads * rows
    dma = pltpu.SemaphoreType.DMA
    hbm = pl.BlockSpec(memory_space=pl.ANY)
    return pl.pallas_call(
        functools.partial(project_kernel, spans, heads),
        out_shape=jax.ShapeDtypeStruct((3, tokens, width), jnp.bfloat16),
        in_specs=[hbm] * 4,
        out_specs=pl.BlockSpec(memory_space=pltpu.VMEM),
        scratch_shapes=[
            pltpu.VMEM((spans, heads, rows, depth), jnp.bfloat16),
            pltpu.VMEM((3, depth, width), jnp.bfloat16),
            pltpu.VMEM((spans, 3, tokens, width), jnp.bfloat16),
            pltpu.VMEM((spans + 1, 3, tokens, width), jnp.bfloat16),
            pltpu.VMEM((3, tokens, width), jnp.float32),
            dma((3,)), dma, dma((spans,)), dma((spans,)),
            dma((spans, heads)), dma((spans, heads)),
            dma((spans, 3)), dma((spans + 1, 3)),
        ],
        compiler_params=pltpu.CompilerParams(collective_id=0, has_side_effects=True),
        name="project",
    )(x, w_query, w_key, w_value)


def unit(block):
    floated = block.astype(jnp.float32)
    norm = jnp.sqrt(jnp.sum(floated * floated, axis=-1, keepdims=True) + 1e-06)
    return (floated / norm).astype(jnp.bfloat16)


def attend_kernel(
    spans, heads, qkv_ref, cum_ref, cum_t_ref, total_ref, near_ref, far_ref, w_ref, out_ref,
    weight, part, inbox, mixed, heads_out, query, keys, state, state_out, state_in, totals,
    w_sem, s_send, s_recv, t_own, t_send, t_recv, g_send, g_recv,
):
    me, lane = lax.axis_index("ctx"), lax.axis_index("head")
    rows = out_ref.shape[0]
    chunks, chunk = part.shape[0], part.shape[-1]
    local_heads, per_span = state.shape[0], qkv_ref.shape[1] // BLOCK
    bits, span_bits = bits_of(heads), bits_of(spans)
    loads = [
        pltpu.make_async_copy(w_ref.at[:, pl.ds(j * chunk, chunk)], weight.at[j], w_sem.at[j])
        for j in range(chunks)
    ]
    own_total = pltpu.make_async_copy(total_ref, totals.at[me], t_own)
    own_total.start()
    for load in loads:
        load.start()
    barrier = pltpu.get_barrier_semaphore()
    for ahead in range(1, spans):
        pl.semaphore_signal(barrier, inc=1, device_id={"ctx": lax.rem(me + ahead, spans)}, device_id_type=MESH)
    for bit in bits:
        pl.semaphore_signal(barrier, inc=1, device_id={"head": flipped(lane, bit)}, device_id_type=MESH)
    pl.semaphore_wait(barrier, spans - 1 + len(bits))

    def send_total(ahead):
        return pltpu.make_async_remote_copy(
            src_ref=total_ref, dst_ref=totals.at[me],
            send_sem=t_send.at[ahead], recv_sem=t_recv.at[me],
            device_id={"ctx": lax.rem(me + ahead, spans)}, device_id_type=MESH,
        )

    def take_total(ahead):
        source = lax.rem(me + ahead, spans)
        return pltpu.make_async_remote_copy(
            src_ref=total_ref, dst_ref=totals.at[source],
            send_sem=t_send.at[ahead], recv_sem=t_recv.at[source],
            device_id={"ctx": source}, device_id_type=MESH,
        )

    def send_state(b, head):
        return pltpu.make_async_remote_copy(
            src_ref=state_out.at[b, head], dst_ref=state_in.at[b, head],
            send_sem=g_send.at[b, head], recv_sem=g_recv.at[b, head],
            device_id={"ctx": flipped(me, span_bits[b])}, device_id_type=MESH,
        )

    for ahead in range(1, spans):
        send_total(ahead).start()

    def lanes(head):
        return slice(head * HEAD_DIM, (head + 1) * HEAD_DIM)

    for head in range(local_heads):
        key = unit(qkv_ref[1, :, lanes(head)])
        keys[head] = key
        fade = jnp.exp(total_ref[head : head + 1, :] - cum_t_ref[:, head : head + 1])
        decayed = (key.astype(jnp.float32) * fade).astype(jnp.bfloat16)
        state[head] = lax.dot_general(
            decayed, qkv_ref[2, :, lanes(head)], (((0,), (0,)), ((), ())), preferred_element_type=jnp.float32
        )
        if span_bits:
            state_out[0, head] = state[head].astype(jnp.bfloat16)
            send_state(0, head).start()

    def near(head):
        query[head] = unit(qkv_ref[0, :, lanes(head)])
        key = keys[head]
        for a in range(per_span):
            at = slice(a * BLOCK, (a + 1) * BLOCK)
            near_out = None
            for e in range(a + 1):
                of = slice(e * BLOCK, (e + 1) * BLOCK)
                scores = lax.dot_general(
                    query[head, at, :], key[of, :], (((1,), (1,)), ((), ())), preferred_element_type=jnp.float32
                )
                spread = cum_t_ref[at, head : head + 1] - cum_ref[head : head + 1, of]
                if e == a:
                    causal = lax.broadcasted_iota(jnp.int32, (BLOCK, BLOCK), 0) >= lax.broadcasted_iota(
                        jnp.int32, (BLOCK, BLOCK), 1
                    )
                    decay = jnp.where(causal, jnp.exp(jnp.where(causal, spread, 0.0)), 0.0)
                else:
                    decay = jnp.exp(spread)
                shaped = (scores * decay * near_ref[(head * per_span + a) * per_span + e]).astype(jnp.bfloat16)
                term = jnp.dot(shaped, qkv_ref[2, of, lanes(head)], preferred_element_type=jnp.float32)
                near_out = term if near_out is None else near_out + term
            mixed[head, at, :] = near_out

    def group_total(place, size):
        start = (place // size) * size
        result = totals[start]
        for i in range(1, size):
            result = result + totals[start + i]
        return result

    split = (local_heads + 1) // 2
    for head in range(split):
        near(head)
    own_total.wait()
    for ahead in range(1, spans):
        take_total(ahead).wait_recv()
    before = jnp.zeros_like(total_ref[...])
    for b, size in enumerate(span_bits):
        upper = (me // size) % 2 == 1
        other_total = group_total(flipped(me, size), size)
        higher = jnp.exp(jnp.where(upper, group_total(me, size), other_total))
        for head in range(local_heads):
            send_state(b, head).wait_recv()
            if b + 1 < len(span_bits):
                other, held = state_in[b, head].astype(jnp.float32), state[head]
                lower_state = jnp.where(upper, other, held)
                higher_state = jnp.where(upper, held, other)
                state[head] = higher[head : head + 1, :] * lower_state + higher_state
                state_out[b + 1, head] = state[head].astype(jnp.bfloat16)
                send_state(b + 1, head).start()
        if b == 0:
            for head in range(split, local_heads):
                near(head)
        for head in range(local_heads):
            reach = jnp.exp(cum_t_ref[:, head : head + 1] + before[head : head + 1, :])
            scaled = (query[head].astype(jnp.float32) * reach).astype(jnp.bfloat16)
            far = jnp.dot(scaled, state_in[b, head], preferred_element_type=jnp.float32)
            for a in range(per_span):
                at = slice(a * BLOCK, (a + 1) * BLOCK)
                gain = jnp.where(upper, far_ref[(a * local_heads + head) * len(span_bits) + b], 0.0)
                mixed[head, at, :] = mixed[head, at, :] + far[at, :] * gain
        before = before + jnp.where(upper, other_total, 0.0)
    for head in range(local_heads):
        heads_out[:, lanes(head)] = mixed[head].astype(jnp.bfloat16)

    orders = [bits[:1] + bits[1:], bits[:1] + bits[:0:-1]]

    def transfer(j, phase, mask):
        bit = orders[j % 2][phase]
        return pltpu.make_async_remote_copy(
            src_ref=part.at[j, flipped(lane, mask | bit)], dst_ref=inbox.at[j, phase, mask],
            send_sem=s_send.at[j, phase, mask], recv_sem=s_recv.at[j, phase, mask],
            device_id={"head": flipped(lane, bit)}, device_id_type=MESH,
        )

    def advance(j, phase):
        path = orders[j % 2]
        if phase == 0:
            loads[j].wait()
            product = jnp.dot(heads_out[...], weight[j], preferred_element_type=jnp.float32)
            part[j] = product.reshape(heads, rows, chunk).astype(jnp.bfloat16)
        else:
            for mask in subsets(path[phase:]):
                transfer(j, phase - 1, mask).wait_recv()
                place = flipped(lane, mask)
                added = part[j, place].astype(jnp.float32) + inbox[j, phase - 1, mask].astype(jnp.float32)
                if phase < len(bits):
                    part[j, place] = added.astype(jnp.bfloat16)
                else:
                    out_ref[:, pl.ds(j * chunk, chunk)] = added.astype(jnp.bfloat16)
        if phase < len(bits):
            for mask in subsets(path[phase + 1 :]):
                transfer(j, phase, mask).start()

    for j in range(chunks):
        advance(j, 0)
    for wave in range(chunks + len(bits) - 1):
        for phase in range(len(bits), 0, -1):
            if 0 <= wave + 1 - phase < chunks:
                advance(wave + 1 - phase, phase)
    for j in range(chunks):
        for phase in range(len(bits)):
            for mask in subsets(orders[j % 2][phase + 1 :]):
                transfer(j, phase, mask).wait_send()
    for ahead in range(1, spans):
        send_total(ahead).wait_send()
    for b in range(len(span_bits)):
        for head in range(local_heads):
            send_state(b, head).wait_send()


def attend(qkv, cum, near_block, far_block, w_out):
    spans, heads = lax.axis_size("ctx"), lax.axis_size("head")
    tokens, width = qkv.shape[1:]
    local_heads = cum.shape[0]
    model = w_out.shape[1]
    rows = tokens // heads
    chunks = 4
    chunk = model // chunks
    phases, rounds = heads.bit_length() - 1, spans.bit_length() - 1
    dma = pltpu.SemaphoreType.DMA
    vmem = pl.BlockSpec(memory_space=pltpu.VMEM)
    smem = pl.BlockSpec(memory_space=pltpu.SMEM)
    totals = jnp.broadcast_to(cum[:, -1:], (local_heads, HEAD_DIM))
    head_state = (local_heads, HEAD_DIM, HEAD_DIM)
    return pl.pallas_call(
        functools.partial(attend_kernel, spans, heads),
        out_shape=jax.ShapeDtypeStruct((rows, model), jnp.bfloat16),
        in_specs=[vmem, vmem, vmem, vmem, smem, smem, pl.BlockSpec(memory_space=pl.ANY)],
        out_specs=vmem,
        scratch_shapes=[
            pltpu.VMEM((chunks, width, chunk), jnp.bfloat16),
            pltpu.VMEM((chunks, heads, rows, chunk), jnp.bfloat16),
            pltpu.VMEM((chunks, phases, heads, rows, chunk), jnp.bfloat16),
            pltpu.VMEM((local_heads, tokens, HEAD_DIM), jnp.float32),
            pltpu.VMEM((tokens, width), jnp.bfloat16),
            pltpu.VMEM((local_heads, tokens, HEAD_DIM), jnp.bfloat16),
            pltpu.VMEM((local_heads, tokens, HEAD_DIM), jnp.bfloat16),
            pltpu.VMEM(head_state, jnp.float32),
            pltpu.VMEM((rounds, *head_state), jnp.bfloat16),
            pltpu.VMEM((rounds, *head_state), jnp.bfloat16),
            pltpu.VMEM((spans, local_heads, HEAD_DIM), jnp.float32),
            dma((chunks,)), dma((chunks, phases, heads)), dma((chunks, phases, heads)),
            dma, dma((spans,)), dma((spans,)),
            dma((rounds, local_heads)), dma((rounds, local_heads)),
        ],
        compiler_params=pltpu.CompilerParams(collective_id=1, has_side_effects=True),
        name="attend",
    )(qkv, cum, cum.T, totals, near_block.reshape(-1), far_block.reshape(-1), w_out)


def levels_of(first, second, count):
    mixed = jnp.bitwise_xor(first, second)
    result = jnp.zeros(mixed.shape, jnp.int32)
    for level_bit in range(count):
        result = result + (mixed >= 2**level_bit).astype(jnp.int32)
    return result


def on_device(layer_input, w_query, w_key, w_value, w_out, log_decay, level_gain, level_mask):
    qkv = project(layer_input, w_query, w_key, w_value)
    cum = jnp.cumsum(log_decay, axis=1)
    level_count = level_gain.shape[1]
    per_span = log_decay.shape[1] // BLOCK
    ctx_index = lax.axis_index("ctx")
    blocks = ctx_index * per_span + jnp.arange(per_span, dtype=jnp.int32)
    level_range = jnp.arange(level_count, dtype=jnp.int32)
    powers = jnp.array(bits_of(lax.axis_size("ctx")), jnp.int32)
    partner = jnp.bitwise_xor(ctx_index, powers)
    block_weight = level_mask.astype(jnp.float32)[:, None, :] * level_gain[None, :, :]
    near_levels = levels_of(blocks[:, None], blocks[None, :], level_count)
    near_onehot = (near_levels[..., None] == level_range).astype(jnp.float32)
    near_block = jnp.sum(block_weight[:, :, None, :] * near_onehot[:, None, :, :], axis=-1)
    far_levels = levels_of(blocks[:, None], (partner * per_span)[None, :], level_count)
    far_onehot = (far_levels[..., None] == level_range).astype(jnp.float32)
    far_block = jnp.sum(block_weight[:, :, None, :] * far_onehot[:, None, :, :], axis=-1)
    return attend(qkv, cum, near_block.transpose(1, 0, 2), far_block, w_out)


def solution(mesh):
    in_specs = (
        P(("ctx", "head"), None),
        P("ctx", "head"),
        P("ctx", "head"),
        P("ctx", "head"),
        P("head", None),
        P("head", "ctx"),
        P("head", None),
        P("ctx", None),
    )
    out_specs = P(("ctx", "head"), None)
    return jax.shard_map(
        on_device, mesh=mesh, in_specs=in_specs, out_specs=out_specs, check_vma=False
    )
```

```python
import functools

import jax
import jax.numpy as jnp
from jax import lax
from jax.experimental import pallas as pl
from jax.experimental.pallas import tpu as pltpu
from jax.sharding import PartitionSpec as P

HEAD_DIM = 128
BLOCK = 128
MESH = pl.DeviceIdType.MESH


def flipped(index, mask):
    bit = 1
    while bit <= mask:
        if mask & bit:
            index = index + bit - 2 * bit * ((index // bit) % 2)
        bit *= 2
    return index


def subsets(bits):
    masks = [0]
    for bit in bits:
        masks = masks + [mask | bit for mask in masks]
    return masks


def bits_of(count):
    return [2**k for k in range(count.bit_length() - 1)]


def visit(step, me, count):
    after, before = count - 1 - me, me
    extra = jnp.abs(after - before)
    more_after = after > before
    turn = step - extra
    half = turn // 2
    from_end = count - 1 - jnp.where(more_after, extra, 0) - half
    from_start = jnp.where(more_after, 0, extra) + half
    even = turn % 2 == 0
    paired = jnp.where(even == more_after, from_start, from_end)
    lone = jnp.where(more_after, count - 1 - step, step)
    return jnp.where(step < extra, lone, paired)


def project_kernel(
    spans, heads, x_ref, wq_ref, wk_ref, wv_ref, out_ref,
    xs, weight, part, inbox, total,
    w_sem, own_sem, z_send, z_recv, g_send, g_recv, p_send, p_recv,
):
    me, lane = lax.axis_index("ctx"), lax.axis_index("head")
    rows = x_ref.shape[0]
    depth, width = weight.shape[1:]
    bits = bits_of(heads)
    order = [visit(step, me, spans) for step in range(spans - 1)]
    sources = (wq_ref, wk_ref, wv_ref)
    loads = [pltpu.make_async_copy(ref, weight.at[k], w_sem.at[k]) for k, ref in enumerate(sources)]

    def columns(span):
        return x_ref.at[:, pl.ds(pl.multiple_of(span * depth, depth), depth)]

    own = pltpu.make_async_copy(columns(me), xs.at[me, lane], own_sem)
    own.start()
    for load in loads:
        load.start()
    barrier = pltpu.get_barrier_semaphore()
    for ahead in range(1, spans):
        pl.semaphore_signal(barrier, inc=1, device_id={"ctx": lax.rem(me + ahead, spans)}, device_id_type=MESH)
    for bit in bits:
        pl.semaphore_signal(barrier, inc=1, device_id={"head": flipped(lane, bit)}, device_id_type=MESH)
    pl.semaphore_wait(barrier, spans - 1 + len(bits))

    def exchange(span, source):
        return pltpu.make_async_remote_copy(
            src_ref=columns(span), dst_ref=xs.at[source, lane],
            send_sem=z_send.at[span], recv_sem=z_recv.at[source],
            device_id={"ctx": span}, device_id_type=MESH,
        )

    for span in order:
        exchange(span, me).start()

    def gather(span, mask, bit):
        block = xs.at[span, flipped(lane, mask)]
        return pltpu.make_async_remote_copy(
            src_ref=block, dst_ref=block,
            send_sem=g_send.at[span, mask | bit], recv_sem=g_recv.at[span, mask | bit],
            device_id={"head": flipped(lane, bit)}, device_id_type=MESH,
        )

    def settled(span, mask):
        block = xs.at[span, flipped(lane, mask)]
        return pltpu.make_async_remote_copy(
            src_ref=block, dst_ref=block,
            send_sem=g_send.at[span, mask], recv_sem=g_recv.at[span, mask],
            device_id={"head": flipped(lane, bits[0])}, device_id_type=MESH,
        )

    def to_right(span, k):
        return pltpu.make_async_remote_copy(
            src_ref=part.at[span, k], dst_ref=inbox.at[span, k],
            send_sem=p_send.at[span, k], recv_sem=p_recv.at[span, k],
            device_id={"ctx": lax.rem(me + 1, spans)}, device_id_type=MESH,
        )

    def to_left(span, k):
        slot = jnp.where(span == me - 1, spans, span)
        return pltpu.make_async_remote_copy(
            src_ref=part.at[span, k], dst_ref=inbox.at[slot, k],
            send_sem=p_send.at[span, k], recv_sem=p_recv.at[slot, k],
            device_id={"ctx": lax.rem(me + spans - 1, spans)}, device_id_type=MESH,
        )

    def landed(slot, k):
        pltpu.make_async_remote_copy(
            src_ref=inbox.at[slot, k], dst_ref=inbox.at[slot, k],
            send_sem=p_send.at[0, k], recv_sem=p_recv.at[slot, k],
            device_id={"ctx": lax.rem(me + 1, spans)}, device_id_type=MESH,
        ).wait_recv()

    def product(span, k):
        block = xs[span]
        if rows % 16:
            block = block.astype(jnp.float32)
        block = block.reshape(heads * rows, depth).astype(jnp.bfloat16)
        return jnp.dot(block, weight[k], preferred_element_type=jnp.float32)

    queue = [me] + order
    orders = [bits[1:] + bits[:1], bits[:0:-1] + bits[:1]]

    def advance(place, phase):
        span, path = queue[place], orders[place % 2]
        if phase == 0:
            if place == 0:
                own.wait()
            else:
                exchange(span, span).wait_recv()
        else:
            for mask in subsets(path[: phase - 1]):
                settled(span, mask | path[phase - 1]).wait_recv()
        if phase < len(bits):
            for mask in subsets(path[:phase]):
                gather(span, mask, path[phase]).start()

    def compute(place):
        span = queue[place]
        for k in range(3):
            if place == 1:
                loads[k].wait()
            part[span, k] = product(span, k).astype(jnp.bfloat16)

            @pl.when((span > me) & (me == 0))
            def _():
                to_right(span, k).start()

            @pl.when((span < me) & (me == spans - 1))
            def _():
                to_left(span, k).start()

    for wave in range(spans + len(bits)):
        for phase in range(len(bits), -1, -1):
            place = wave - phase
            if 0 <= place < spans:
                advance(place, phase)
                if phase == len(bits) and place > 0:
                    compute(place)
    for k in range(3):
        total[k] = product(me, k)
    for span in order:
        for k in range(3):

            @pl.when((span > me) & (me > 0))
            def _():
                landed(span, k)
                part[span, k] = (part[span, k].astype(jnp.float32) + inbox[span, k].astype(jnp.float32)).astype(jnp.bfloat16)
                to_right(span, k).start()

            @pl.when((span < me) & (me < spans - 1))
            def _():
                landed(span, k)
                part[span, k] = (part[span, k].astype(jnp.float32) + inbox[span, k].astype(jnp.float32)).astype(jnp.bfloat16)
                to_left(span, k).start()

    for k in range(3):

        @pl.when(me > 0)
        def _():
            landed(me, k)
            total[k] = total[k] + inbox[me, k].astype(jnp.float32)

        @pl.when(me < spans - 1)
        def _():
            landed(spans, k)
            total[k] = total[k] + inbox[spans, k].astype(jnp.float32)

        out_ref[k] = total[k].astype(jnp.bfloat16)
    for span in order:
        exchange(span, me).wait_send()
        for k in range(3):
            to_right(span, k).wait_send()
    for span in queue:
        for mask in range(1, heads):
            settled(span, mask).wait_send()


def project(x, w_query, w_key, w_value):
    spans, heads = lax.axis_size("ctx"), lax.axis_size("head")
    rows = x.shape[0]
    depth, width = w_query.shape
    tokens = heads * rows
    dma = pltpu.SemaphoreType.DMA
    hbm = pl.BlockSpec(memory_space=pl.ANY)
    return pl.pallas_call(
        functools.partial(project_kernel, spans, heads),
        out_shape=jax.ShapeDtypeStruct((3, tokens, width), jnp.bfloat16),
        in_specs=[hbm] * 4,
        out_specs=pl.BlockSpec(memory_space=pltpu.VMEM),
        scratch_shapes=[
            pltpu.VMEM((spans, heads, rows, depth), jnp.bfloat16),
            pltpu.VMEM((3, depth, width), jnp.bfloat16),
            pltpu.VMEM((spans, 3, tokens, width), jnp.bfloat16),
            pltpu.VMEM((spans + 1, 3, tokens, width), jnp.bfloat16),
            pltpu.VMEM((3, tokens, width), jnp.float32),
            dma((3,)), dma, dma((spans,)), dma((spans,)),
            dma((spans, heads)), dma((spans, heads)),
            dma((spans, 3)), dma((spans + 1, 3)),
        ],
        compiler_params=pltpu.CompilerParams(collective_id=0, has_side_effects=True),
        name="project",
    )(x, w_query, w_key, w_value)


def unit(block):
    floated = block.astype(jnp.float32)
    norm = jnp.sqrt(jnp.sum(floated * floated, axis=-1, keepdims=True) + 1e-06)
    return (floated / norm).astype(jnp.bfloat16)


def attend_kernel(
    spans, heads, qkv_ref, decay_ref, gain_ref, mask_ref, w_ref, out_ref,
    weight, part, inbox, mixed, heads_out, query, keys, state, state_out, state_in, totals,
    cum_ref, cum_t_ref, total_ref,
    w_sem, s_send, s_recv, t_own, t_send, t_recv, g_send, g_recv,
):
    me, lane = lax.axis_index("ctx"), lax.axis_index("head")
    rows = out_ref.shape[0]
    chunks, chunk = part.shape[0], part.shape[-1]
    local_heads, per_span = state.shape[0], qkv_ref.shape[1] // BLOCK
    bits, span_bits = bits_of(heads), bits_of(spans)
    loads = [
        pltpu.make_async_copy(w_ref.at[:, pl.ds(j * chunk, chunk)], weight.at[j], w_sem.at[j])
        for j in range(chunks)
    ]
    for load in loads:
        load.start()
    tokens = qkv_ref.shape[1]
    earlier = lax.broadcasted_iota(jnp.int32, (tokens, tokens), 1) <= lax.broadcasted_iota(
        jnp.int32, (tokens, tokens), 0
    )
    decays = decay_ref[...]

    def summed(first, second):
        return lax.dot_general(
            first, second, (((1,), (1,)), ((), ())),
            precision=lax.Precision.HIGHEST, preferred_element_type=jnp.float32,
        )

    cum_ref[...] = summed(decays, earlier.astype(jnp.float32))
    cum_t_ref[...] = summed(earlier.astype(jnp.float32), decays)
    total_ref[...] = summed(decays, jnp.ones((HEAD_DIM, tokens), jnp.float32))
    level_count = gain_ref.shape[1]

    def level_weight(head, a, mixed_blocks):
        level = mixed_blocks.bit_length()
        if level >= level_count:
            return jnp.float32(0)
        return gain_ref[head, level] * mask_ref[a, level].astype(jnp.float32)

    own_total = pltpu.make_async_copy(total_ref, totals.at[me], t_own)
    own_total.start()
    barrier = pltpu.get_barrier_semaphore()
    for ahead in range(1, spans):
        pl.semaphore_signal(barrier, inc=1, device_id={"ctx": lax.rem(me + ahead, spans)}, device_id_type=MESH)
    for bit in bits:
        pl.semaphore_signal(barrier, inc=1, device_id={"head": flipped(lane, bit)}, device_id_type=MESH)
    pl.semaphore_wait(barrier, spans - 1 + len(bits))

    def send_total(ahead):
        return pltpu.make_async_remote_copy(
            src_ref=total_ref, dst_ref=totals.at[me],
            send_sem=t_send.at[ahead], recv_sem=t_recv.at[me],
            device_id={"ctx": lax.rem(me + ahead, spans)}, device_id_type=MESH,
        )

    def take_total(ahead):
        source = lax.rem(me + ahead, spans)
        return pltpu.make_async_remote_copy(
            src_ref=total_ref, dst_ref=totals.at[source],
            send_sem=t_send.at[ahead], recv_sem=t_recv.at[source],
            device_id={"ctx": source}, device_id_type=MESH,
        )

    def send_state(b, head):
        return pltpu.make_async_remote_copy(
            src_ref=state_out.at[b, head], dst_ref=state_in.at[b, head],
            send_sem=g_send.at[b, head], recv_sem=g_recv.at[b, head],
            device_id={"ctx": flipped(me, span_bits[b])}, device_id_type=MESH,
        )

    for ahead in range(1, spans):
        send_total(ahead).start()

    def lanes(head):
        return slice(head * HEAD_DIM, (head + 1) * HEAD_DIM)

    for head in range(local_heads):
        key = unit(qkv_ref[1, :, lanes(head)])
        keys[head] = key
        fade = jnp.exp(total_ref[head : head + 1, :] - cum_t_ref[:, head : head + 1])
        decayed = (key.astype(jnp.float32) * fade).astype(jnp.bfloat16)
        state[head] = lax.dot_general(
            decayed, qkv_ref[2, :, lanes(head)], (((0,), (0,)), ((), ())), preferred_element_type=jnp.float32
        )
        if span_bits:
            state_out[0, head] = state[head].astype(jnp.bfloat16)
            send_state(0, head).start()

    def near(head):
        query[head] = unit(qkv_ref[0, :, lanes(head)])
        key = keys[head]
        for a in range(per_span):
            at = slice(a * BLOCK, (a + 1) * BLOCK)
            near_out = None
            for e in range(a + 1):
                of = slice(e * BLOCK, (e + 1) * BLOCK)
                scores = lax.dot_general(
                    query[head, at, :], key[of, :], (((1,), (1,)), ((), ())), preferred_element_type=jnp.float32
                )
                spread = cum_t_ref[at, head : head + 1] - cum_ref[head : head + 1, of]
                if e == a:
                    causal = lax.broadcasted_iota(jnp.int32, (BLOCK, BLOCK), 0) >= lax.broadcasted_iota(
                        jnp.int32, (BLOCK, BLOCK), 1
                    )
                    decay = jnp.where(causal, jnp.exp(jnp.where(causal, spread, 0.0)), 0.0)
                else:
                    decay = jnp.exp(spread)
                shaped = (scores * decay * level_weight(head, a, a ^ e)).astype(jnp.bfloat16)
                term = jnp.dot(shaped, qkv_ref[2, of, lanes(head)], preferred_element_type=jnp.float32)
                near_out = term if near_out is None else near_out + term
            mixed[head, at, :] = near_out

    def group_total(place, size):
        start = (place // size) * size
        result = totals[start]
        for i in range(1, size):
            result = result + totals[start + i]
        return result

    split = (local_heads + 1) // 2
    for head in range(split):
        near(head)
    own_total.wait()
    for ahead in range(1, spans):
        take_total(ahead).wait_recv()
    before = jnp.zeros_like(total_ref[...])
    for b, size in enumerate(span_bits):
        upper = (me // size) % 2 == 1
        other_total = group_total(flipped(me, size), size)
        higher = jnp.exp(jnp.where(upper, group_total(me, size), other_total))
        for head in range(local_heads):
            send_state(b, head).wait_recv()
            if b + 1 < len(span_bits):
                other, held = state_in[b, head].astype(jnp.float32), state[head]
                lower_state = jnp.where(upper, other, held)
                higher_state = jnp.where(upper, held, other)
                state[head] = higher[head : head + 1, :] * lower_state + higher_state
                state_out[b + 1, head] = state[head].astype(jnp.bfloat16)
                send_state(b + 1, head).start()
        if b == 0:
            for head in range(split, local_heads):
                near(head)
        for head in range(local_heads):
            reach = jnp.exp(cum_t_ref[:, head : head + 1] + before[head : head + 1, :])
            scaled = (query[head].astype(jnp.float32) * reach).astype(jnp.bfloat16)
            far = jnp.dot(scaled, state_in[b, head], preferred_element_type=jnp.float32)
            for a in range(per_span):
                at = slice(a * BLOCK, (a + 1) * BLOCK)
                gain = jnp.where(upper, level_weight(head, a, size * per_span + a), 0.0)
                mixed[head, at, :] = mixed[head, at, :] + far[at, :] * gain
        before = before + jnp.where(upper, other_total, 0.0)
    for head in range(local_heads):
        heads_out[:, lanes(head)] = mixed[head].astype(jnp.bfloat16)

    orders = [bits[:1] + bits[1:], bits[:1] + bits[:0:-1]]

    def transfer(j, phase, mask):
        bit = orders[j % 2][phase]
        return pltpu.make_async_remote_copy(
            src_ref=part.at[j, flipped(lane, mask | bit)], dst_ref=inbox.at[j, mask | bit],
            send_sem=s_send.at[j, mask | bit], recv_sem=s_recv.at[j, mask | bit],
            device_id={"head": flipped(lane, bit)}, device_id_type=MESH,
        )

    def advance(j, phase):
        path = orders[j % 2]
        if phase == 0:
            loads[j].wait()
            product = jnp.dot(heads_out[...], weight[j], preferred_element_type=jnp.float32)
            part[j] = product.reshape(heads, rows, chunk).astype(jnp.bfloat16)
        else:
            for mask in subsets(path[phase:]):
                transfer(j, phase - 1, mask).wait_recv()
                place = flipped(lane, mask)
                added = part[j, place].astype(jnp.float32) + inbox[j, mask | path[phase - 1]].astype(jnp.float32)
                if phase < len(bits):
                    part[j, place] = added.astype(jnp.bfloat16)
                else:
                    out_ref[:, pl.ds(j * chunk, chunk)] = added.astype(jnp.bfloat16)
        if phase < len(bits):
            for mask in subsets(path[phase + 1 :]):
                transfer(j, phase, mask).start()

    for j in range(chunks):
        advance(j, 0)
    for wave in range(chunks + len(bits) - 1):
        for phase in range(len(bits), 0, -1):
            if 0 <= wave + 1 - phase < chunks:
                advance(wave + 1 - phase, phase)
    for j in range(chunks):
        for phase in range(len(bits)):
            for mask in subsets(orders[j % 2][phase + 1 :]):
                transfer(j, phase, mask).wait_send()
    for ahead in range(1, spans):
        send_total(ahead).wait_send()
    for b in range(len(span_bits)):
        for head in range(local_heads):
            send_state(b, head).wait_send()


def attend(qkv, log_decay, level_gain, level_mask, w_out):
    spans, heads = lax.axis_size("ctx"), lax.axis_size("head")
    tokens, width = qkv.shape[1:]
    local_heads = log_decay.shape[0]
    model = w_out.shape[1]
    rows = tokens // heads
    chunks = 8
    chunk = model // chunks
    rounds = spans.bit_length() - 1
    dma = pltpu.SemaphoreType.DMA
    vmem = pl.BlockSpec(memory_space=pltpu.VMEM)
    smem = pl.BlockSpec(memory_space=pltpu.SMEM)
    head_state = (local_heads, HEAD_DIM, HEAD_DIM)
    return pl.pallas_call(
        functools.partial(attend_kernel, spans, heads),
        out_shape=jax.ShapeDtypeStruct((rows, model), jnp.bfloat16),
        in_specs=[vmem, vmem, smem, smem, pl.BlockSpec(memory_space=pl.ANY)],
        out_specs=vmem,
        scratch_shapes=[
            pltpu.VMEM((chunks, width, chunk), jnp.bfloat16),
            pltpu.VMEM((chunks, heads, rows, chunk), jnp.bfloat16),
            pltpu.VMEM((chunks, heads, rows, chunk), jnp.bfloat16),
            pltpu.VMEM((local_heads, tokens, HEAD_DIM), jnp.float32),
            pltpu.VMEM((tokens, width), jnp.bfloat16),
            pltpu.VMEM((local_heads, tokens, HEAD_DIM), jnp.bfloat16),
            pltpu.VMEM((local_heads, tokens, HEAD_DIM), jnp.bfloat16),
            pltpu.VMEM(head_state, jnp.float32),
            pltpu.VMEM((rounds, *head_state), jnp.bfloat16),
            pltpu.VMEM((rounds, *head_state), jnp.bfloat16),
            pltpu.VMEM((spans, local_heads, HEAD_DIM), jnp.float32),
            pltpu.VMEM((local_heads, tokens), jnp.float32),
            pltpu.VMEM((tokens, local_heads), jnp.float32),
            pltpu.VMEM((local_heads, HEAD_DIM), jnp.float32),
            dma((chunks,)), dma((chunks, heads)), dma((chunks, heads)),
            dma, dma((spans,)), dma((spans,)),
            dma((rounds, local_heads)), dma((rounds, local_heads)),
        ],
        compiler_params=pltpu.CompilerParams(collective_id=1, has_side_effects=True),
        name="attend",
    )(qkv, log_decay, level_gain, level_mask, w_out)


def on_device(layer_input, w_query, w_key, w_value, w_out, log_decay, level_gain, level_mask):
    qkv = project(layer_input, w_query, w_key, w_value)
    return attend(qkv, log_decay, level_gain, level_mask, w_out)


def solution(mesh):
    in_specs = (
        P(("ctx", "head"), None),
        P("ctx", "head"),
        P("ctx", "head"),
        P("ctx", "head"),
        P("head", None),
        P("head", "ctx"),
        P("head", None),
        P("ctx", None),
    )
    out_specs = P(("ctx", "head"), None)
    return jax.shard_map(
        on_device, mesh=mesh, in_specs=in_specs, out_specs=out_specs, check_vma=False
    )
```
